32 devices in a mesh: table: 8 (over z, y), helper: 4 (over x, core).
Axes of the slice: x: 2, y: 2, z: 4, core: 2. Of those that a mesh axis runs over, the one named last changes fastest.
Arguments:
- tables: bfloat16 [64, 4096, 128], P('table'), may hold values from -6 to 6
- projections: bfloat16 [64, 128, 256], P('table'), may hold values from -0.0234375 to 0.0234375
- bag_rows: int32 [64, 8, 4, 8, 16], P('table', None, 'helper'), may hold values from 0 to 4095
- bag_lengths: int32 [64, 8, 4, 8], P('table', None, 'helper'), may hold values from 1 to 16
- candidates: bfloat16 [8, 4, 2048, 256], P('table', 'helper'), may hold values from -6 to 6
- request_counts: int32 [8, 4, 8], P('table', 'helper'), may hold values from 1 to 1024, as said below
- cross_down: bfloat16 [3, 512, 128], replicated, may hold values from -0.25 to 0.25
- cross_up: bfloat16 [3, 128, 512], replicated, may hold values from -0.5 to 0.5
- cross_bias: float32 [3, 512], replicated, may hold values from -3 to 3
- layer_one: bfloat16 [512, 1024], replicated, may hold values from -0.25 to 0.25
- bias_one: float32 [1024], replicated, may hold values from -2 to 2
- layer_two: bfloat16 [1024, 512], replicated, may hold values from -0.1875 to 0.1875
- bias_two: float32 [512], replicated, may hold values from -2 to 2
- layer_three: bfloat16 [512, 256], replicated, may hold values from -0.25 to 0.25
- bias_three: float32 [256], replicated, may hold values from -2 to 2
- score_weight: bfloat16 [256], replicated, may hold values from -0.375 to 0.375
Outputs:
- scores: float32 [8, 4, 2048], P('table', 'helper')
The draws below stay inside these ranges and needn't reach their ends.
Inputs may be any that keep to these rules, and one draw needn't show every extreme that they name: For each (a, h) the 8 counts request_counts[a, h, :] sum to at most 2048; for every a exactly one h has a sum of exactly 2048, and in that list the first request holds exactly 1024 candidates.
All inputs are finite; a program needn't handle non-finite values.
Results may differ from the reference program's by a relative error of at most 0.018.
Values may be sent and summed in bfloat16 or wider, within the bound.
A program may use at most 128 MiB of HBM per device.

```python
import math
import jax
import jax.numpy as jnp
import numpy as np
from jax import lax

E = 128
P_SIZE = 256
RANK = 128
H1 = 1024
H2 = 512
H3 = 256
ROWS = 4096
CROSS = 3
BLOCK = 256
BAG = 16
REQ_DEV = 8
BLK_DEV = 8
NTAB = 64
SLOTS = 2048
D0 = 512
N_TABLE = 8
N_HELPER = 4


def split_total(key, totals, parts):
    shares = jax.random.randint(key, totals.shape + (parts,), 1, 5)
    running = jnp.cumsum(shares, axis=-1)
    ends = totals[..., None] * running // running[..., -1:]
    starts = jnp.concatenate([jnp.zeros_like(ends[..., :1]), ends[..., :-1]], axis=-1)
    return (ends - starts).astype(jnp.int32)


def draw_request_counts(key, part):
    first, second, third, fourth = jax.random.split(jax.random.fold_in(key, 11), 4)
    lowest = max(BLOCK // 2, 4 * REQ_DEV)
    highest = SLOTS // 2
    totals = jax.random.randint(first, (N_TABLE, N_HELPER), lowest, highest + 1)
    fullest = jax.random.randint(second, (N_TABLE,), 0, N_HELPER)
    helpers = jnp.arange(N_HELPER, dtype=jnp.int32)
    is_full = helpers[None, :] == fullest[:, None]
    drawn = split_total(third, totals, REQ_DEV)
    if REQ_DEV == 1:
        full_counts = jnp.full((N_TABLE, N_HELPER, 1), SLOTS, jnp.int32)
    else:
        leading = SLOTS // 2
        rest = split_total(fourth, jnp.full((N_TABLE, N_HELPER), SLOTS - leading, jnp.int32), REQ_DEV - 1)
        full_counts = jnp.concatenate([jnp.full((N_TABLE, N_HELPER, 1), leading, jnp.int32), rest], axis=-1)
    return jnp.where(is_full[..., None], full_counts, drawn).astype(jnp.int32)


def touch_ends(values, stream_key, low, largest):
    longest = values.shape.index(max(values.shape))
    spots = []
    for shift in (0, 1):
        where = [jax.random.randint(jax.random.fold_in(stream_key, axis), (), 0, length) for axis, length in enumerate(values.shape)]
        where[longest] = (where[longest] + shift) % values.shape[longest]
        spots.append(tuple(where))
    return values.at[spots[0]].set(low).at[spots[1]].set(largest)


def level_of(rng, extent, cuts, least, high):
    def one(dim, shards_of):
        draws = jax.random.uniform(jax.random.fold_in(jax.random.fold_in(rng, 6), dim), (shards_of,), jnp.float32, least / len(cuts), high / len(cuts))
        return jnp.repeat(jnp.exp(draws), extent[dim] // shards_of).reshape((-1,) + (1,) * (len(extent) - dim - 1))

    factor_of = one(*cuts[0])
    for cut in cuts[1:]:
        factor_of = factor_of * one(*cut)
    return factor_of


def cumulative_ranks(amount, slope):
    portions = [(1 << 20) // math.isqrt(standing ** slope) + 1 for standing in range(1, amount + 1)]
    spread = 1 + sum(portions) // (1 << 30)
    return np.cumsum(np.array([max(1, weight // spread) for weight in portions]))


def ranked(stream_key, extent, number_of, lean):
    table = cumulative_ranks(number_of, lean)
    lot = jax.random.randint(jax.random.fold_in(stream_key, 1), extent, 0, int(table[number_of - 1]))
    rank = jnp.searchsorted(jnp.asarray(table, jnp.int32), lot, side="right")
    return jax.random.permutation(jax.random.fold_in(stream_key, 2), number_of)[rank].astype(jnp.int32)


def scatter_about(stream_key, dims, spread, limit, cuts=(), kind=jnp.bfloat16):
    entries = jax.random.normal(stream_key, dims, jnp.float32) * spread
    if len(cuts) > 0:
        entries = level_of(stream_key, dims, cuts, -0.22, 0.18) * entries
    return jnp.clip(entries, min=-limit, max=limit).astype(kind)


def setup_inputs(seed: int = 0) -> dict:
    arg_keys = jax.random.split(jax.random.key(seed), 17)
    tables = scatter_about(arg_keys[0], (NTAB, ROWS, E), 1.0, 6.0, ((0, 8),))
    projections = scatter_about(arg_keys[1], (NTAB, E, P_SIZE), (E * BAG * NTAB // 2) ** -0.5, 0.0234375, ((0, 8),))
    bag_rows = touch_ends(ranked(arg_keys[2], (NTAB, N_TABLE, N_HELPER, REQ_DEV, BAG), ROWS, 2), jax.random.fold_in(arg_keys[2], 3), 0, ROWS - 1).astype(jnp.int32)
    bag_lengths = touch_ends(jax.random.randint(arg_keys[3], (NTAB, N_TABLE, N_HELPER, REQ_DEV), 1, BAG + 1), jax.random.fold_in(arg_keys[3], 1), 1, BAG).astype(jnp.int32)
    candidates = scatter_about(arg_keys[4], (N_TABLE, N_HELPER, SLOTS, P_SIZE), 1.0, 6.0, ((0, 8), (1, 4)))
    request_counts = draw_request_counts(jax.random.fold_in(arg_keys[16], 71), 0)
    cross_down = scatter_about(arg_keys[6], (CROSS, D0, RANK), D0 ** -0.5, 0.25)
    cross_up = scatter_about(arg_keys[7], (CROSS, RANK, D0), RANK ** -0.5, 0.5)
    cross_bias = scatter_about(arg_keys[8], (CROSS, D0), 0.5, 3.0, (), jnp.float32)
    layer_one = scatter_about(arg_keys[9], (D0, H1), D0 ** -0.5, 0.25)
    bias_one = scatter_about(arg_keys[10], (H1,), 0.3, 2.0, (), jnp.float32)
    layer_two = scatter_about(arg_keys[11], (H1, H2), H1 ** -0.5, 0.1875)
    bias_two = scatter_about(arg_keys[12], (H2,), 0.3, 2.0, (), jnp.float32)
    layer_three = scatter_about(arg_keys[13], (H2, H3), H2 ** -0.5, 0.25)
    bias_three = scatter_about(arg_keys[14], (H3,), 0.3, 2.0, (), jnp.float32)
    score_weight = scatter_about(arg_keys[15], (H3,), H3 ** -0.5, 0.375)
    return {"tables": tables, "projections": projections, "bag_rows": bag_rows, "bag_lengths": bag_lengths, "candidates": candidates, "request_counts": request_counts, "cross_down": cross_down, "cross_up": cross_up, "cross_bias": cross_bias, "layer_one": layer_one, "bias_one": bias_one, "layer_two": layer_two, "bias_two": bias_two, "layer_three": layer_three, "bias_three": bias_three, "score_weight": score_weight}


def cross_network(features, context_rows, live_slots, weights):
    cross_down, cross_up, cross_bias, layer_one, bias_one, layer_two, bias_two, layer_three, bias_three, score_weight = weights
    cross_input = jnp.concatenate([features, context_rows], axis=1)
    anchor = cross_input.astype(jnp.float32)
    current = anchor
    for layer_number in range(cross_down.shape[0]):
        reduced = jnp.dot(current.astype(jnp.bfloat16), cross_down[layer_number], preferred_element_type=jnp.float32).astype(jnp.bfloat16)
        current = anchor * (jnp.dot(reduced, cross_up[layer_number], preferred_element_type=jnp.float32) + cross_bias[layer_number]) + current
    hidden = jax.nn.relu(jnp.dot(current.astype(jnp.bfloat16), layer_one, preferred_element_type=jnp.float32) + bias_one).astype(jnp.bfloat16)
    hidden = jax.nn.relu(jnp.dot(hidden, layer_two, preferred_element_type=jnp.float32) + bias_two).astype(jnp.bfloat16)
    hidden = jax.nn.relu(jnp.dot(hidden, layer_three, preferred_element_type=jnp.float32) + bias_three).astype(jnp.bfloat16)
    result = jnp.dot(hidden, score_weight, preferred_element_type=jnp.float32)
    return jnp.where(live_slots, result, jnp.zeros_like(result))


def block_scores(features, codes, context, weights):
    labels = jnp.arange(context.shape[0], dtype=jnp.int32)
    choose = (codes[:, None] == labels[None, :]).astype(jnp.bfloat16)
    context_rows = jnp.dot(choose, context, preferred_element_type=jnp.float32).astype(jnp.bfloat16)
    return cross_network(features, context_rows, codes >= 0, weights)


def slot_codes(counts, total_slots):
    ends = jnp.cumsum(counts)
    positions = jnp.arange(total_slots, dtype=jnp.int32)
    owner = jnp.sum((positions[:, None] >= ends[None, :]).astype(jnp.int32), axis=1)
    return jnp.where(owner < counts.shape[0], owner, -1).astype(jnp.int32)


def reference(tables, projections, bag_rows, bag_lengths, candidates, request_counts, cross_down, cross_up, cross_bias, layer_one, bias_one, layer_two, bias_two, layer_three, bias_three, score_weight):
    weights = (cross_down, cross_up, cross_bias, layer_one, bias_one, layer_two, bias_two, layer_three, bias_three, score_weight)

    def add_table(total, pieces):
        table, projection, indices, lengths = pieces
        looked = table[indices]
        keep = jnp.arange(indices.shape[-1], dtype=jnp.int32) < lengths[..., None]
        pooled = jnp.sum(jnp.where(keep[..., None], looked, jnp.zeros_like(looked)), axis=-2, dtype=jnp.float32).astype(jnp.bfloat16)
        projected = jnp.dot(pooled.reshape(-1, pooled.shape[-1]), projection, preferred_element_type=jnp.float32).astype(jnp.bfloat16)
        projected = lax.optimization_barrier(projected)
        return total + projected.astype(jnp.float32).reshape(total.shape), None

    start = jnp.zeros((N_TABLE, N_HELPER, REQ_DEV, P_SIZE), jnp.float32)
    total, ignored = lax.scan(add_table, start, (tables, projections, bag_rows, bag_lengths))
    context = total.astype(jnp.bfloat16)
    codes = jax.vmap(jax.vmap(lambda counts: slot_codes(counts, SLOTS)))(request_counts)
    count_blocks = N_TABLE * N_HELPER * BLK_DEV
    feature_blocks = candidates.reshape(count_blocks, BLOCK, P_SIZE)
    code_blocks = codes.reshape(count_blocks, BLOCK)
    context_blocks = jnp.repeat(context.reshape(N_TABLE * N_HELPER, REQ_DEV, P_SIZE), BLK_DEV, axis=0)

    def one_block(pieces):
        features, block_codes, block_context = pieces
        return lax.cond(block_codes[0] >= 0,
                        lambda: block_scores(features, block_codes, block_context, weights),
                        lambda: jnp.zeros((BLOCK,), jnp.float32))

    scores = lax.map(one_block, (feature_blocks, code_blocks, context_blocks))
    return scores.reshape(N_TABLE, N_HELPER, SLOTS)
```

```python
import functools

import jax
import jax.numpy as jnp
from jax import lax
from jax.experimental import pallas as pl
from jax.experimental.pallas import tpu as pltpu
from jax.sharding import PartitionSpec as P

GROUP = 16
SUB = 256
CHAINS = 2


def lane_dot(left, right):
    return lax.dot_general(
        left, right, (((1,), (1,)), ((), ())), preferred_element_type=jnp.float32
    )


def dot(left, right):
    return jnp.dot(left, right, preferred_element_type=jnp.float32)


def kernel(
    peers,
    bag,
    counts_ref,
    hi_ref,
    lo_ref,
    tables_hbm,
    proj_hbm,
    cand_hbm,
    down_hbm,
    up_hbm,
    one_hbm,
    two_hbm,
    three_hbm,
    cross_bias_ref,
    bias_one_ref,
    bias_two_ref,
    bias_three_ref,
    score_ref,
    out_ref,
    tables_v,
    proj_v,
    cand_v,
    down_v,
    up_v,
    one_v,
    two_v,
    three_v,
    tally,
    send,
    recv,
    context_v,
    table_sem,
    load_sem,
    send_sem,
    recv_sem,
):
    me = lax.axis_index("table")
    local_tables, rows, width = tables_v.shape
    requests = send.shape[1]
    bags = peers * requests
    groups = bags // GROUP
    lo_size = 256
    hi_size = rows // lo_size
    slots = cand_v.shape[0]

    loads = [
        pltpu.make_async_copy(source, target, load_sem.at[number])
        for number, (source, target) in enumerate(
            (
                (proj_hbm, proj_v),
                (cand_hbm, cand_v),
                (down_hbm, down_v),
                (up_hbm, up_v),
                (one_hbm, one_v),
                (two_hbm, two_v),
                (three_hbm, three_v),
            )
        )
    ]

    def table_copy(number):
        return pltpu.make_async_copy(
            tables_hbm.at[number], tables_v.at[number], table_sem.at[number]
        )

    for number in range(local_tables):
        table_copy(number).start()
    for load in loads:
        load.start()

    barrier = pltpu.get_barrier_semaphore()

    def greet(step, carry):
        peer = lax.rem(me + step, peers)
        pl.semaphore_signal(barrier, inc=1, device_id={"table": peer})
        return carry

    lax.fori_loop(1, peers, greet, 0)

    hi_labels = lax.broadcasted_iota(jnp.int32, (hi_size * GROUP, GROUP * bag), 0).astype(
        jnp.float32
    ).astype(jnp.bfloat16)
    lo_labels = lax.broadcasted_iota(jnp.int32, (lo_size, GROUP * bag), 0).astype(
        jnp.float32
    ).astype(jnp.bfloat16)
    one = jnp.ones((), jnp.bfloat16)
    zero = jnp.zeros((), jnp.bfloat16)

    loads[0].wait()
    total = jnp.zeros((bags, proj_v.shape[2]), jnp.float32)
    for number in range(local_tables):
        for group in range(groups):
            hi = hi_ref[number, pl.ds(group, 1), :]
            lo = lo_ref[number, pl.ds(group, 1), :]
            left = jnp.where(hi_labels == hi, one, zero)
            right = jnp.where(lo_labels == lo, one, zero)
            part = lane_dot(left, right).astype(jnp.bfloat16)
            for high in range(hi_size):
                tally[
                    number % 2,
                    pl.ds(group * GROUP, GROUP),
                    pl.ds(high * lo_size, lo_size),
                ] = part[high * GROUP : (high + 1) * GROUP]
        table_copy(number).wait()
        pooled = dot(tally[number % 2], tables_v[number]).astype(jnp.bfloat16)
        total = total + dot(pooled, proj_v[number])
    send[...] = total.reshape(send.shape)

    pl.semaphore_wait(barrier, peers - 1)

    def remote(step):
        peer = lax.rem(me + step, peers)
        return pltpu.make_async_remote_copy(
            src_ref=send.at[peer],
            dst_ref=recv.at[step],
            send_sem=send_sem.at[step],
            recv_sem=recv_sem.at[step],
            device_id={"table": peer},
        )

    def start(step, carry):
        remote(step).start()
        return carry

    def finish(step, summed):
        remote(step).wait()
        return summed + recv[step]

    lax.fori_loop(1, peers, start, 0)
    for load in loads[1:]:
        load.wait()
    summed = lax.fori_loop(1, peers, finish, send[me])
    context_v[...] = summed.astype(jnp.bfloat16)

    lanes = lax.broadcasted_iota(jnp.int32, (1, requests), 1)
    starts = jnp.zeros((1, requests), jnp.int32)
    ends = jnp.zeros((1, requests), jnp.int32)
    live_total = 0
    for request in range(requests):
        count = counts_ref[0, 0, request]
        starts = starts + jnp.where(lanes > request, count, 0)
        ends = ends + jnp.where(lanes >= request, count, 0)
        live_total = live_total + count

    def tower(first):
        slot = first + lax.broadcasted_iota(jnp.int32, (SUB, requests), 0)
        choose = jnp.where((slot >= starts) & (slot < ends), 1.0, 0.0).astype(jnp.bfloat16)
        context_rows = dot(choose, context_v[...])
        features = cand_v[pl.ds(first, SUB), :].astype(jnp.float32)
        anchor = jnp.concatenate([features, context_rows], axis=1)
        current = anchor
        for layer in range(down_v.shape[0]):
            reduced = dot(current.astype(jnp.bfloat16), down_v[layer]).astype(jnp.bfloat16)
            current = (
                anchor * (dot(reduced, up_v[layer]) + cross_bias_ref[layer : layer + 1, :])
                + current
            )
        hidden = jnp.maximum(
            dot(current.astype(jnp.bfloat16), one_v[...]) + bias_one_ref[...], 0.0
        ).astype(jnp.bfloat16)
        hidden = jnp.maximum(dot(hidden, two_v[...]) + bias_two_ref[...], 0.0).astype(
            jnp.bfloat16
        )
        hidden = jnp.maximum(dot(hidden, three_v[...]) + bias_three_ref[...], 0.0).astype(
            jnp.bfloat16
        )
        result = lane_dot(score_ref[...], hidden)
        position = first + lax.broadcasted_iota(jnp.int32, (1, SUB), 1)
        out_ref[:, pl.ds(first, SUB)] = jnp.where(position < live_total, result, 0.0)

    def step(number, carry):
        for chain in range(CHAINS):
            tower(pl.multiple_of((number * CHAINS + chain) * SUB, SUB))
        return carry

    lax.fori_loop(0, slots // (SUB * CHAINS), step, 0)


def body(
    peers,
    tables,
    projections,
    bag_rows,
    bag_lengths,
    candidates,
    request_counts,
    cross_down,
    cross_up,
    cross_bias,
    layer_one,
    bias_one,
    layer_two,
    bias_two,
    layer_three,
    bias_three,
    score_weight,
):
    local_tables, rows, width = tables.shape
    owners, requests, bag = bag_rows.shape[1], bag_rows.shape[3], bag_rows.shape[4]
    groups = owners * requests // GROUP
    features = candidates[0, 0]
    slots, pwidth = features.shape
    keep = jnp.arange(bag, dtype=jnp.int32) < bag_lengths[..., None]
    bag_number = jnp.arange(owners * requests, dtype=jnp.int32).reshape(owners, 1, requests, 1)
    hi = jnp.where(keep, (bag_rows // 256) * GROUP + bag_number % GROUP, -1)
    lo = bag_rows % 256
    hi = hi.astype(jnp.bfloat16).reshape(local_tables, groups, GROUP * bag)
    lo = lo.astype(jnp.bfloat16).reshape(local_tables, groups, GROUP * bag)
    vmem = pl.BlockSpec(memory_space=pltpu.VMEM)
    hbm = pl.BlockSpec(memory_space=pl.ANY)
    smem = pl.BlockSpec(memory_space=pltpu.SMEM)
    big = (tables, projections, features, cross_down, cross_up, layer_one, layer_two, layer_three)
    scores = pl.pallas_call(
        functools.partial(kernel, peers, bag),
        out_shape=jax.ShapeDtypeStruct((1, slots), jnp.float32),
        in_specs=[smem, vmem, vmem] + [hbm] * 8 + [vmem] * 5,
        out_specs=vmem,
        scratch_shapes=[pltpu.VMEM(array.shape, array.dtype) for array in big]
        + [
            pltpu.VMEM((2, owners * requests, rows), jnp.bfloat16),
            pltpu.VMEM((owners, requests, pwidth), jnp.float32),
            pltpu.VMEM((owners, requests, pwidth), jnp.float32),
            pltpu.VMEM((requests, pwidth), jnp.bfloat16),
            pltpu.SemaphoreType.DMA((local_tables,)),
            pltpu.SemaphoreType.DMA((7,)),
            pltpu.SemaphoreType.DMA((owners,)),
            pltpu.SemaphoreType.DMA((owners,)),
        ],
        compiler_params=pltpu.CompilerParams(
            collective_id=0, has_side_effects=True, vmem_limit_bytes=60 * 1024 * 1024
        ),
        name="rank_step",
    )(
        request_counts,
        hi,
        lo,
        *big,
        cross_bias,
        bias_one.reshape(1, -1),
        bias_two.reshape(1, -1),
        bias_three.reshape(1, -1),
        score_weight.reshape(1, -1),
    )
    return scores.reshape(1, 1, slots)


def solution(mesh):
    in_specs = (
        P("table", None, None),
        P("table", None, None),
        P("table", None, "helper", None, None),
        P("table", None, "helper", None),
        P("table", "helper", None, None),
        P("table", "helper", None),
    ) + (P(),) * 10
    out_specs = P("table", "helper", None)
    return jax.shard_map(
        functools.partial(body, mesh.shape["table"]),
        mesh=mesh,
        in_specs=in_specs,
        out_specs=out_specs,
        check_vma=False,
    )
```

```python
import functools

import jax
import jax.numpy as jnp
from jax import lax
from jax.experimental import pallas as pl
from jax.experimental.pallas import tpu as pltpu
from jax.sharding import PartitionSpec as P

DEPTH = 256
TALLY_BYTES = 8 << 20
SUB = 1024
CHAINS = 1


def lane_dot(left, right):
    return lax.dot_general(
        left, right, (((1,), (1,)), ((), ())), preferred_element_type=jnp.float32
    )


def dot(left, right):
    return jnp.dot(left, right, preferred_element_type=jnp.float32)


def kernel(
    peers,
    bag,
    counts_hbm,
    rows_hbm,
    lengths_hbm,
    tables_hbm,
    proj_hbm,
    cand_hbm,
    down_hbm,
    up_hbm,
    one_hbm,
    two_hbm,
    three_hbm,
    cross_bias_hbm,
    bias_one_hbm,
    bias_two_hbm,
    bias_three_hbm,
    score_hbm,
    out_ref,
    counts_ref,
    rows_ref,
    lengths_ref,
    tables_v,
    proj_v,
    cand_v,
    down_v,
    up_v,
    one_v,
    two_v,
    three_v,
    cross_bias_ref,
    bias_one_ref,
    bias_two_ref,
    bias_three_ref,
    score_ref,
    hi_v,
    lo_v,
    tally,
    send,
    recv,
    context_v,
    table_sem,
    load_sem,
    send_sem,
    recv_sem,
):
    me = lax.axis_index("table")
    local_tables, rows, width = tables_v.shape
    requests = send.shape[1]
    bags = peers * requests
    together = DEPTH // (requests * bag)
    group_bags = together * requests
    groups = peers // together
    lo_size = 256
    hi_size = rows // lo_size
    slots = cand_v.shape[0]

    def copies(pairs, offset):
        return [
            pltpu.make_async_copy(source, target, load_sem.at[offset + number])
            for number, (source, target) in enumerate(pairs)
        ]

    first_loads = copies(((rows_hbm, rows_ref), (lengths_hbm, lengths_ref), (proj_hbm, proj_v)), 0)
    late_loads = copies(
        (
            (counts_hbm, counts_ref),
            (cand_hbm, cand_v),
            (down_hbm, down_v),
            (up_hbm, up_v),
            (one_hbm, one_v),
            (two_hbm, two_v),
            (three_hbm, three_v),
            (cross_bias_hbm, cross_bias_ref),
            (bias_one_hbm, bias_one_ref),
            (bias_two_hbm, bias_two_ref),
            (bias_three_hbm, bias_three_ref),
            (score_hbm, score_ref),
        ),
        3,
    )

    def table_copy(number):
        return pltpu.make_async_copy(
            tables_hbm.at[number], tables_v.at[number], table_sem.at[number]
        )

    for load in first_loads:
        load.start()
    for number in range(local_tables):
        table_copy(number).start()

    def code_rows():
        span = requests * bag
        raw = rows_ref[...]
        pick = lax.broadcasted_iota(jnp.int32, (bag, span), 0)
        lane = lax.broadcasted_iota(jnp.int32, (bag, span), 1)
        spread = jnp.where(pick == lane % bag, 1.0, 0.0).astype(jnp.bfloat16)
        pick = lax.broadcasted_iota(jnp.int32, (requests, span), 0)
        lane = lax.broadcasted_iota(jnp.int32, (requests, span), 1)
        own = pick == lane // bag
        spread_lengths = jnp.where(own, 1.0, 0.0).astype(jnp.bfloat16)

        def flat(values):
            wide = dot(values.astype(jnp.float32).astype(jnp.bfloat16), spread)
            wide = wide.reshape(values.shape[0] // requests, requests, span)
            return jnp.sum(jnp.where(own[None], wide, 0.0), axis=1)

        hi = flat(raw // lo_size)
        lo = flat(raw % lo_size)
        lengths = dot(lengths_ref[...].astype(jnp.float32).astype(jnp.bfloat16), spread_lengths)
        lane = lax.broadcasted_iota(jnp.int32, hi.shape, 1)
        line = lax.broadcasted_iota(jnp.int32, hi.shape, 0)
        place = (line % together) * requests + lane // bag
        keep = (lane % bag).astype(jnp.float32) < lengths
        hi_v[...] = jnp.where(keep, hi * group_bags + place.astype(jnp.float32), -1.0)
        lo_v[...] = lo

    def joined(source, first):
        pieces = [source[pl.ds(first + n, 1), :] for n in range(together)]
        return jnp.concatenate(pieces, axis=1).astype(jnp.bfloat16)

    barrier = pltpu.get_barrier_semaphore()

    def greet(step, carry):
        peer = lax.rem(me + step, peers)
        pl.semaphore_signal(barrier, inc=1, device_id={"table": peer})
        return carry

    lax.fori_loop(1, peers, greet, 0)

    for load in first_loads:
        load.wait()
    code_rows()

    def labels(count):
        numbers = lax.broadcasted_iota(jnp.int32, (count, DEPTH), 0)
        return numbers.astype(jnp.float32).astype(jnp.bfloat16)

    hi_labels = labels(hi_size * group_bags)
    lo_labels = labels(lo_size)
    one = jnp.ones((), jnp.bfloat16)
    zero = jnp.zeros((), jnp.bfloat16)

    def fill(number):
        for group in range(groups):
            first = number * peers + group * together
            hi = joined(hi_v, first)
            lo = joined(lo_v, first)
            left = jnp.where(hi_labels == hi, one, zero)
            right = jnp.where(lo_labels == lo, one, zero)
            part = lane_dot(left, right).astype(jnp.bfloat16)
            for high in range(hi_size):
                tally[
                    number % tally.shape[0],
                    pl.ds(group * group_bags, group_bags),
                    pl.ds(high * lo_size, lo_size),
                ] = part[high * group_bags : (high + 1) * group_bags]

    ahead = tally.shape[0]
    for number in range(ahead):
        fill(number)
    total = jnp.zeros((bags, proj_v.shape[2]), jnp.float32)
    for number in range(local_tables):
        table_copy(number).wait()
        pooled = dot(tally[number % tally.shape[0]], tables_v[number]).astype(jnp.bfloat16)
        total = total + dot(pooled, proj_v[number])
        if number + ahead < local_tables:
            fill(number + ahead)
    send[...] = total.reshape(send.shape)

    pl.semaphore_wait(barrier, peers - 1)

    def remote(step):
        peer = lax.rem(me + step, peers)
        return pltpu.make_async_remote_copy(
            src_ref=send.at[peer],
            dst_ref=recv.at[step],
            send_sem=send_sem.at[step],
            recv_sem=recv_sem.at[step],
            device_id={"table": peer},
        )

    def start(step, carry):
        remote(step).start()
        return carry

    def finish(step, summed):
        remote(step).wait()
        return summed + recv[step]

    lax.fori_loop(1, peers, start, 0)
    for load in late_loads:
        load.start()
    for load in late_loads:
        load.wait()
    summed = lax.fori_loop(1, peers, finish, send[me])
    context_v[...] = summed.astype(jnp.bfloat16)

    lanes = lax.broadcasted_iota(jnp.int32, (1, requests), 1)
    starts = jnp.zeros((1, requests), jnp.int32)
    ends = jnp.zeros((1, requests), jnp.int32)
    live_total = 0
    for request in range(requests):
        count = counts_ref[0, 0, request]
        starts = starts + jnp.where(lanes > request, count, 0)
        ends = ends + jnp.where(lanes >= request, count, 0)
        live_total = live_total + count

    def tower(first):
        slot = first + lax.broadcasted_iota(jnp.int32, (SUB, requests), 0)
        choose = jnp.where((slot >= starts) & (slot < ends), 1.0, 0.0).astype(jnp.bfloat16)
        context_rows = dot(choose, context_v[...])
        features = cand_v[pl.ds(first, SUB), :].astype(jnp.float32)
        anchor = jnp.concatenate([features, context_rows], axis=1)
        current = anchor
        for layer in range(down_v.shape[0]):
            reduced = dot(current.astype(jnp.bfloat16), down_v[layer]).astype(jnp.bfloat16)
            current = (
                anchor * (dot(reduced, up_v[layer]) + cross_bias_ref[layer : layer + 1, :])
                + current
            )
        hidden = jnp.maximum(
            dot(current.astype(jnp.bfloat16), one_v[...]) + bias_one_ref[...], 0.0
        ).astype(jnp.bfloat16)
        hidden = jnp.maximum(dot(hidden, two_v[...]) + bias_two_ref[...], 0.0).astype(
            jnp.bfloat16
        )
        hidden = jnp.maximum(dot(hidden, three_v[...]) + bias_three_ref[...], 0.0).astype(
            jnp.bfloat16
        )
        result = lane_dot(score_ref[...].reshape(1, -1), hidden)
        position = first + lax.broadcasted_iota(jnp.int32, (1, SUB), 1)
        out_ref[:, pl.ds(first, SUB)] = jnp.where(position < live_total, result, 0.0)

    def step(number, carry):
        for chain in range(CHAINS):
            tower(pl.multiple_of((number * CHAINS + chain) * SUB, SUB))
        return carry

    lax.fori_loop(0, slots // (SUB * CHAINS), step, 0)


def body(
    peers,
    tables,
    projections,
    bag_rows,
    bag_lengths,
    candidates,
    request_counts,
    cross_down,
    cross_up,
    cross_bias,
    layer_one,
    bias_one,
    layer_two,
    bias_two,
    layer_three,
    bias_three,
    score_weight,
):
    local_tables, rows, width = tables.shape
    owners, requests, bag = bag_rows.shape[1], bag_rows.shape[3], bag_rows.shape[4]
    features = candidates[0, 0]
    slots, pwidth = features.shape
    vmem = pl.BlockSpec(memory_space=pltpu.VMEM)
    hbm = pl.BlockSpec(memory_space=pl.ANY)
    operands = (
        request_counts,
        bag_rows.reshape(-1, bag),
        bag_lengths.reshape(-1, requests),
        tables,
        projections,
        features,
        cross_down,
        cross_up,
        layer_one,
        layer_two,
        layer_three,
        cross_bias,
        bias_one.reshape(1, -1),
        bias_two.reshape(1, -1),
        bias_three.reshape(1, -1),
        score_weight,
    )
    room = TALLY_BYTES // (owners * requests * rows * 2)
    ahead = min(local_tables, max(1, room))
    scores = pl.pallas_call(
        functools.partial(kernel, peers, bag),
        out_shape=jax.ShapeDtypeStruct((1, slots), jnp.float32),
        in_specs=[hbm] * len(operands),
        out_specs=vmem,
        scratch_shapes=[pltpu.SMEM(request_counts.shape, jnp.int32)]
        + [pltpu.VMEM(array.shape, array.dtype) for array in operands[1:]]
        + [
            pltpu.VMEM((local_tables * owners, requests * bag), jnp.float32),
            pltpu.VMEM((local_tables * owners, requests * bag), jnp.float32),
            pltpu.VMEM((ahead, owners * requests, rows), jnp.bfloat16),
            pltpu.VMEM((owners, requests, pwidth), jnp.float32),
            pltpu.VMEM((owners, requests, pwidth), jnp.float32),
            pltpu.VMEM((requests, pwidth), jnp.bfloat16),
            pltpu.SemaphoreType.DMA((local_tables,)),
            pltpu.SemaphoreType.DMA((len(operands) - 1,)),
            pltpu.SemaphoreType.DMA((owners,)),
            pltpu.SemaphoreType.DMA((owners,)),
        ],
        compiler_params=pltpu.CompilerParams(
            collective_id=0, has_side_effects=True, vmem_limit_bytes=60 * 1024 * 1024
        ),
        name="rank_step",
    )(*operands)
    return scores.reshape(1, 1, slots)


def solution(mesh):
    in_specs = (
        P("table", None, None),
        P("table", None, None),
        P("table", None, "helper", None, None),
        P("table", None, "helper", None),
        P("table", "helper", None, None),
        P("table", "helper", None),
    ) + (P(),) * 10
    out_specs = P("table", "helper", None)
    return jax.shard_map(
        functools.partial(body, mesh.shape["table"]),
        mesh=mesh,
        in_specs=in_specs,
        out_specs=out_specs,
        check_vma=False,
    )
```
